32 devices in a mesh: src: 8 (over y, x, core), tgt: 4 (over z).
Axes of the slice: x: 2, y: 2, z: 4, core: 2. Of those that a mesh axis runs over, the one named last changes fastest.
Arguments:
- src_emb: bfloat16 [64, 131072], P(None, 'src'), may hold values from -3 to 3
- tgt_emb: bfloat16 [64, 65536], P(None, 'tgt'), may hold values from -3 to 3
- src_hidden: bfloat16 [64, 131072], P(None, 'src'), may hold values from -4 to 4
- growth: float32 [131072], P('src'), may hold values from -1 to 1
- tgt_mass: float32 [65536], P('tgt'), may hold values from 0.5 to 2
- pair_code: int32 [8, 4, 512], P('src', 'tgt'), may hold values from 0 to 16383, as said below
- pair_count: int32 [8, 4], P('src', 'tgt'), may hold values from 128 to 512, as said below
- block_batch: int32 [1024], P('src'), may hold values from 0 to 31
Outputs:
- src_potential: float32 [131072], P('src')
- tgt_potential: float32 [65536], P('tgt')
- tgt_grad: float32 [64, 65536], P(None, 'tgt')
- adapter_grad: float32 [32, 64, 64], P(('src', 'tgt'))
The draws below stay inside these ranges and needn't reach their ends.
Inputs may be any that keep to these rules, and one draw needn't show every extreme that they name: `pair_code`: the codes of one device are distinct; among the first 128 entries of each device's list every one of its 128 source blocks and every one of its 128 target blocks appears. `pair_count`: in every draw some device has all 512 entries live.
All inputs are finite; a program needn't handle non-finite values.
Results may differ from the reference program's by a relative error of at most 0.0003.
Values sent between devices are 32-bit elements; how exact they have to be, the bound alone decides.
A program may use at most 192 MiB of HBM per device.

```python
import math
import jax
import jax.numpy as jnp
from jax import lax

D = 64
BLK = 128
SB = 128
TB = 128
PAIRS = 512
ITERS = 2
NS = 131072
NT = 65536
NSB = 1024
NTB = 512
ENC = 32
N_SRC = 8
N_TGT = 4


def draw_one_list(key):
    perm_key, shift_key = jax.random.split(key)
    covered = max(SB, TB)
    offset = jax.random.randint(shift_key, (), 0, TB)
    ranking = jax.random.permutation(perm_key, SB * TB).astype(jnp.int32)
    position = jnp.arange(covered, dtype=jnp.int32)
    cover_codes = position % SB * TB + (position + offset) % TB
    scores = ranking + SB * TB
    scores = scores.at[cover_codes].set(ranking[cover_codes])
    ordering = jnp.argsort(scores)
    return ordering[:PAIRS].astype(jnp.int32)


def draw_pair_code(key, part):
    keys = jax.random.split(jax.random.fold_in(key, 11), N_SRC * N_TGT)
    lists = jax.vmap(draw_one_list)(keys)
    return lists.reshape(N_SRC, N_TGT, PAIRS).astype(jnp.int32)


def draw_pair_count(key, part):
    count_key, full_key = jax.random.split(jax.random.fold_in(key, 23))
    covered = max(SB, TB)
    counts = jax.random.randint(count_key, (N_SRC * N_TGT,), covered, PAIRS // 2 + 1)
    busiest = jax.random.randint(full_key, (), 0, N_SRC * N_TGT)
    counts = jnp.where(jnp.arange(N_SRC * N_TGT) == busiest, PAIRS, counts)
    return counts.astype(jnp.int32).reshape(N_SRC, N_TGT)


def plant(values, stream_key, least, high):
    longest = values.shape.index(max(values.shape))
    spots = []
    for shift in (0, 1):
        where = [jax.random.randint(jax.random.fold_in(stream_key, axis), (), 0, length) for axis, length in enumerate(values.shape)]
        where[longest] = (where[longest] + shift) % values.shape[longest]
        spots.append(tuple(where))
    return values.at[spots[0]].set(least).at[spots[1]].set(high)


def shard_levels(key, dims, shards, low, high):
    gain, own = 1.0, jax.random.fold_in(key, 6)
    for dim, parts in shards:
        draws = jnp.exp(jax.random.uniform(jax.random.fold_in(own, dim), (parts,), jnp.float32, low / len(shards), high / len(shards)))
        gain = gain * jnp.repeat(draws, dims[dim] // parts).reshape([-1 if axis == dim else 1 for axis in range(len(dims))])
    return gain


def centred(rng, extent, spread, most, pieces=(), kind=jnp.bfloat16):
    values = jax.random.normal(rng, extent, jnp.float32) * spread
    if len(pieces) > 0:
        values = shard_levels(rng, extent, pieces, -0.22, 0.18) * values
    return jnp.clip(values, min=-most, max=most).astype(kind)


def setup_inputs(seed: int = 0) -> dict:
    arg_keys = jax.random.split(jax.random.key(seed), 9)
    src_emb = centred(arg_keys[0], (D, NS), 1.0, 3.0, ((1, 8),))
    tgt_emb = centred(arg_keys[1], (D, NT), 1.0, 3.0, ((1, 4),))
    src_hidden = centred(arg_keys[2], (D, NS), 1.0, 4.0, ((1, 8),))
    growth = jnp.clip(jax.random.uniform(arg_keys[3], (NS,), jnp.float32, -1.0, 1.0) * shard_levels(arg_keys[3], (NS,), ((0, 8),), -0.4, 0.0), -1.0, 1.0)
    tgt_mass = jnp.clip(jnp.exp(math.log(2.0) - 1.3862944 * jax.random.uniform(arg_keys[4], (NT,), jnp.float32) ** shard_levels(arg_keys[4], (NT,), ((0, 4),), -0.2, 0.2)), 0.5, 2.0)
    pair_code = draw_pair_code(jax.random.fold_in(arg_keys[8], 71), 0)
    pair_count = draw_pair_count(jax.random.fold_in(arg_keys[8], 71), 0)
    block_batch = plant(jax.random.randint(arg_keys[7], (NSB,), 0, ENC), jax.random.fold_in(arg_keys[7], 1), 0, ENC - 1).astype(jnp.int32)
    return {"src_emb": src_emb, "tgt_emb": tgt_emb, "src_hidden": src_hidden, "growth": growth, "tgt_mass": tgt_mass, "pair_code": pair_code, "pair_count": pair_count, "block_batch": block_batch}


entropy_scale = 0.5
update_power = 0.4
highest = lax.Precision.HIGHEST

def pair_lists(pair_code, pair_count):
    src_index = jnp.arange(N_SRC, dtype=jnp.int32)[:, None, None] * SB + pair_code // TB
    tgt_index = jnp.arange(N_TGT, dtype=jnp.int32)[None, :, None] * TB + pair_code % TB
    alive_mask = (jnp.arange(PAIRS, dtype=jnp.int32)[None, None, :] < pair_count[:, :, None]).astype(jnp.float32)
    group_size = math.gcd(PAIRS, 64)
    group_count = N_SRC * N_TGT * PAIRS // group_size
    return (src_index.astype(jnp.int32).reshape(group_count, group_size), tgt_index.astype(jnp.int32).reshape(group_count, group_size), alive_mask.reshape(group_count, group_size))

def kernel_blocks(x_blocks, y_blocks, x_norms, y_norms, src_group, tgt_group, alive_group):
    inner_prods = jnp.einsum('dgi,dgj->gij', x_blocks[:, src_group].astype(jnp.float32), y_blocks[:, tgt_group].astype(jnp.float32), precision=highest)
    distance = (x_norms[src_group][:, :, None] + y_norms[tgt_group][:, None, :] - 2.0 * inner_prods) / D
    return jnp.exp(-distance / entropy_scale) * alive_group[:, None, None]

def reference(src_emb, tgt_emb, src_hidden, growth, tgt_mass, pair_code, pair_count, block_batch):
    x_blocks = src_emb.reshape(D, NSB, BLK)
    y_blocks = tgt_emb.reshape(D, NTB, BLK)
    x_norms = lax.optimization_barrier(jnp.sum(jnp.square(x_blocks.astype(jnp.float32)), axis=0))
    y_norms = lax.optimization_barrier(jnp.sum(jnp.square(y_blocks.astype(jnp.float32)), axis=0))
    src_lists, tgt_lists, alive_lists = pair_lists(pair_code, pair_count)
    src_mass = jnp.exp(growth).reshape(NSB, BLK)
    tgt_weight = tgt_mass.reshape(NTB, BLK)
    src_scale = jnp.ones((NSB, BLK), jnp.float32)
    tgt_scale = jnp.ones((NTB, BLK), jnp.float32)
    for iteration in range(ITERS):

        def add_sums(carry, inputs):
            row_total, col_total = carry
            src_group, tgt_group, alive_group = inputs
            kernel = kernel_blocks(x_blocks, y_blocks, x_norms, y_norms, src_group, tgt_group, alive_group)
            row_total = row_total.at[src_group].add(jnp.einsum('gij,gj->gi', kernel, tgt_scale[tgt_group], precision=highest))
            col_total = col_total.at[tgt_group].add(jnp.einsum('gij,gi->gj', kernel, src_scale[src_group], precision=highest))
            return ((row_total, col_total), None)
        start_sums = (jnp.zeros((NSB, BLK), jnp.float32), jnp.zeros((NTB, BLK), jnp.float32))
        (row_sums, col_sums), _ = lax.scan(add_sums, start_sums, (src_lists, tgt_lists, alive_lists))
        src_scale, tgt_scale = (jnp.sqrt(src_scale) * jnp.power(src_mass / row_sums, update_power), jnp.sqrt(tgt_scale) * jnp.power(tgt_weight / col_sums, update_power))

    def gradient_group(carry, inputs):
        dx_total, dy_total = carry
        src_group, tgt_group, alive_group = inputs
        kernel = kernel_blocks(x_blocks, y_blocks, x_norms, y_norms, src_group, tgt_group, alive_group)
        transport = src_scale[src_group][:, :, None] * kernel * tgt_scale[tgt_group][:, None, :]
        plan_bf16 = lax.optimization_barrier(transport.astype(jnp.bfloat16)).astype(jnp.float32)
        x_part = x_blocks[:, src_group].astype(jnp.float32)
        y_part = y_blocks[:, tgt_group].astype(jnp.float32)
        pulled = jnp.einsum('gij,dgj->dgi', plan_bf16, y_part, precision=highest)
        pushed = jnp.einsum('gij,dgi->dgj', plan_bf16, x_part, precision=highest)
        dx_term = lax.optimization_barrier(jnp.sum(transport, axis=2))[None] * x_part - pulled
        dy_term = lax.optimization_barrier(jnp.sum(transport, axis=1))[None] * y_part - pushed
        return ((dx_total.at[:, src_group].add(dx_term), dy_total.at[:, tgt_group].add(dy_term)), None)
    start_grads = (jnp.zeros((D, NSB, BLK), jnp.float32), jnp.zeros((D, NTB, BLK), jnp.float32))
    (dx_total, dy_total), _ = lax.scan(gradient_group, start_grads, (src_lists, tgt_lists, alive_lists))
    src_potential = (entropy_scale * jnp.log(src_scale)).reshape(NS)
    tgt_potential = (entropy_scale * jnp.log(tgt_scale)).reshape(NT)
    hidden_blocks = src_hidden.reshape(D, NSB, BLK).astype(jnp.float32)
    outer = jnp.einsum('dbi,ebi->bde', hidden_blocks, dx_total, precision=highest) / BLK
    adapter_grad = jax.ops.segment_sum(outer, block_batch, num_segments=ENC)
    return (src_potential, tgt_potential, dy_total.reshape(D, NT), adapter_grad)
```

```python
import functools
import math

import jax
import jax.numpy as jnp
from jax import lax
from jax.experimental import pallas as pl
from jax.experimental.pallas import tpu as pltpu
from jax.sharding import PartitionSpec as P

BLK = 128
ENC_DEV = 1
ENTROPY = 0.5
POWER = 0.4
AUG = 16
UNROLL = 8
BF = jnp.bfloat16
F32 = jnp.float32
NT_DIMS = (((1,), (1,)), ((), ()))


def split3(value):
    high = value.astype(BF).astype(F32)
    rest = value - high
    mid = rest.astype(BF).astype(F32)
    return high, mid, rest - mid


def lanes(index):
    return pl.ds(pl.multiple_of(index * BLK, BLK), BLK)


def augment(norm_part, own_first):
    high, mid, low = split3(norm_part)
    row = lax.broadcasted_iota(jnp.int32, (AUG, BLK), 0)
    own = 0 if own_first else 3
    ones = 3 - own
    out = jnp.where((row >= ones) & (row < ones + 3), 1.0, 0.0).astype(F32)
    for place, term in enumerate((high, mid, low)):
        out = jnp.where(row == own + place, term, out)
    return out


def prepare(x_ref, y_ref, src_log, tgt_log, x_aug, y_aug, gain):
    feat = x_ref.shape[0]
    depth = x_aug.shape[1]
    src_blocks = x_ref.shape[1] // BLK
    tgt_blocks = y_ref.shape[1] // BLK

    def term(block, log_ref, index):
        norm = jnp.sum(jnp.square(block), axis=0, keepdims=True)
        value = -0.5 * norm
        if log_ref is not None:
            value = value + log_ref[pl.ds(index, 1), :] * (1.0 / gain)
        return value

    pad = jnp.zeros((depth - feat - AUG, BLK), F32)

    def src_one(index, _):
        block = x_ref[:, lanes(index)].astype(F32)
        full = jnp.concatenate([block, augment(term(block, src_log, index), True), pad], axis=0)
        x_aug[lanes(index), :] = full.T.astype(BF)
        return 0

    def tgt_one(index, _):
        bf_block = y_ref[:, lanes(index)]
        extra = augment(term(bf_block.astype(F32), tgt_log, index), False)
        y_aug[:feat, lanes(index)] = bf_block
        y_aug[feat:, lanes(index)] = jnp.concatenate([extra, pad], axis=0).astype(BF)
        return 0

    lax.fori_loop(0, src_blocks, src_one, 0, unroll=4)
    lax.fori_loop(0, tgt_blocks, tgt_one, 0, unroll=4)
    column = lax.broadcasted_iota(jnp.int32, (BLK, depth), 1)
    x_aug[pl.ds(src_blocks * BLK, BLK), :] = jnp.where(column == feat, -131072.0, 0.0).astype(BF)


def pair_of(code_ref, count, slot, src_blocks, tgt_blocks):
    code = code_ref[slot]
    shift = tgt_blocks.bit_length() - 1
    if tgt_blocks == 1 << shift:
        src_id, tgt_id = lax.shift_right_logical(code, shift), code & (tgt_blocks - 1)
    else:
        src_id, tgt_id = code // tgt_blocks, code % tgt_blocks
    return src_id, tgt_id, jnp.where(slot < count, src_id, src_blocks)


def plan_block(x_aug, y_aug, load_id, tgt_id, gain):
    acc = jnp.dot(x_aug[lanes(load_id), :], y_aug[:, lanes(tgt_id)], preferred_element_type=F32)
    return jnp.exp2(acc * (gain * math.log2(math.e)))


def split_wide(plan):
    high = plan.astype(BF)
    low = (plan - high.astype(F32)).astype(BF)
    return high, jnp.concatenate([high, low], axis=1)


def fold(plan):
    return jnp.sum(plan.reshape(BLK // 8, 8, BLK), axis=0)


def sums_kernel(first, gain, code_ref, count_ref, x_ref, y_ref, *refs):
    src_blocks = x_ref.shape[1] // BLK
    tgt_blocks = y_ref.shape[1] // BLK
    if first:
        row_out, col_out, x_aug, y_aug, row_acc, col_acc = refs
        src_log = tgt_log = None
    else:
        (growth, mass, row_in, col_in, row_out, col_out, src_log, tgt_log, x_aug, y_aug,
         row_acc, col_acc) = refs
        src_log[...] = POWER * (growth[...] - jnp.log(row_in[...]))
        tgt_log[...] = POWER * (jnp.log(mass[...]) - jnp.log(col_in[...]))
    prepare(x_ref, y_ref, src_log, tgt_log, x_aug, y_aug, gain)
    row_acc[...] = jnp.zeros_like(row_acc)
    col_acc[...] = jnp.zeros_like(col_acc)
    count = count_ref[0]
    pick = jnp.where(lax.broadcasted_iota(jnp.int32, (8, 2 * BLK), 0) == 0, 1.0, 0.0).astype(BF)

    def step(group, _):
        parts = []
        for inner in range(UNROLL):
            slot = group * UNROLL + inner
            src_id, tgt_id, load_id = pair_of(code_ref, count, slot, src_blocks, tgt_blocks)
            plan = plan_block(x_aug, y_aug, load_id, tgt_id, gain)
            _, wide = split_wide(plan)
            rows = lax.dot_general(pick, wide, NT_DIMS, preferred_element_type=F32)
            parts.append((src_id, tgt_id, rows, fold(plan)))
        for src_id, tgt_id, rows, cols in parts:
            row_acc[src_id] += rows
            col_acc[tgt_id] += cols
        return 0

    lax.fori_loop(0, (count + UNROLL - 1) // UNROLL, step, 0)
    row_out[...] = jnp.sum(row_acc[...], axis=1)
    col_out[...] = jnp.sum(col_acc[...], axis=1)


def grads_kernel(gain, code_ref, count_ref, batch_ref, x_ref, y_ref, hid_ref, growth, mass,
                 row_in, col_in, src_prev, tgt_prev, src_pot, tgt_pot, dy_ref, adp_ref,
                 src_log, tgt_log, x_aug, y_aug, dx_acc, col_acc):
    feat = x_ref.shape[0]
    src_blocks = x_ref.shape[1] // BLK
    tgt_blocks = y_ref.shape[1] // BLK
    src_new = (0.5 + POWER) * src_prev[...] + POWER * (growth[...] - jnp.log(row_in[...]))
    tgt_new = (0.5 + POWER) * tgt_prev[...] + POWER * (jnp.log(mass[...]) - jnp.log(col_in[...]))
    src_log[...] = src_new
    tgt_log[...] = tgt_new
    src_pot[...] = ENTROPY * src_new
    tgt_pot[...] = ENTROPY * tgt_new
    prepare(x_ref, y_ref, src_log, tgt_log, x_aug, y_aug, gain)
    dx_acc[...] = jnp.zeros_like(dx_acc)
    dy_ref[...] = jnp.zeros_like(dy_ref)
    col_acc[...] = jnp.zeros_like(col_acc)
    adp_ref[...] = jnp.zeros_like(adp_ref)
    count = count_ref[0]
    wide_rows = feat + AUG
    kept = feat + 8
    pick = jnp.where(
        lax.broadcasted_iota(jnp.int32, (wide_rows, BLK), 0) == feat, 1.0, 0.0
    ).astype(BF)
    group_size = UNROLL // 2

    def step(group, _):
        parts = []
        for inner in range(group_size):
            slot = group * group_size + inner
            src_id, tgt_id, load_id = pair_of(code_ref, count, slot, src_blocks, tgt_blocks)
            plan = plan_block(x_aug, y_aug, load_id, tgt_id, gain)
            high, wide = split_wide(plan)
            left = jnp.concatenate([y_aug[:wide_rows, lanes(tgt_id)], pick], axis=1)
            pulled = lax.dot_general(left, wide, NT_DIMS, preferred_element_type=F32)
            pushed = jnp.dot(x_ref[:, lanes(src_id)], high, preferred_element_type=F32)
            parts.append((src_id, tgt_id, pulled[:kept], pushed, fold(plan)))
        for src_id, tgt_id, pulled, pushed, cols in parts:
            dx_acc[src_id] += pulled
            dy_ref[:, lanes(tgt_id)] += pushed
            col_acc[tgt_id] += cols
        return 0

    lax.fori_loop(0, (count + group_size - 1) // group_size, step, 0)

    def finish_tgt(index, _):
        total = jnp.sum(col_acc[index], axis=0, keepdims=True)
        dy_ref[:, lanes(index)] = total * y_ref[:, lanes(index)].astype(F32) - dy_ref[:, lanes(index)]
        return 0

    lax.fori_loop(0, tgt_blocks, finish_tgt, 0, unroll=4)

    def finish_src(group, _):
        parts = []
        for inner in range(4):
            index = group * 4 + inner
            acc = dx_acc[index]
            grad = acc[feat:feat + 1] * x_ref[:, lanes(index)].astype(F32) - acc[:feat]
            _, wide = split_wide(grad)
            hid = hid_ref[:, lanes(index)]
            outer = lax.dot_general(
                jnp.concatenate([hid, hid], axis=1), wide, NT_DIMS, preferred_element_type=F32
            )
            parts.append((batch_ref[index], outer * (1.0 / BLK)))
        for batch, outer in parts:
            adp_ref[batch] += outer
        return 0

    lax.fori_loop(0, src_blocks // 4, finish_src, 0)


def local_calls(slots, feat, src_cells, tgt_cells, owners, interpret=False):
    src_blocks, tgt_blocks = src_cells // BLK, tgt_cells // BLK
    gain = 2.0 / (feat * ENTROPY)
    depth = -(-(feat + AUG) // BLK) * BLK
    smem = pl.BlockSpec(memory_space=pltpu.SMEM)
    vmem = pl.BlockSpec(memory_space=pltpu.VMEM)
    row_shape = jax.ShapeDtypeStruct((src_blocks, BLK), F32)
    col_shape = jax.ShapeDtypeStruct((tgt_blocks, BLK), F32)
    aug = [pltpu.VMEM((src_cells + BLK, depth), BF), pltpu.VMEM((depth, tgt_cells), BF)]
    col_acc = pltpu.VMEM((tgt_blocks, 8, BLK), F32)
    params = pltpu.CompilerParams(vmem_limit_bytes=56 * 1024 * 1024)

    def sums(first):
        scratch = aug + [pltpu.VMEM((src_blocks, 8, BLK), F32), col_acc]
        outs = [row_shape, col_shape] + ([] if first else [row_shape, col_shape])
        return pl.pallas_call(
            functools.partial(sums_kernel, first, gain),
            out_shape=outs,
            in_specs=[smem] * 2 + [vmem] * (2 if first else 6),
            out_specs=[vmem] * len(outs),
            scratch_shapes=scratch,
            compiler_params=params,
            interpret=interpret,
        )

    grads = pl.pallas_call(
        functools.partial(grads_kernel, gain),
        out_shape=[
            row_shape,
            col_shape,
            jax.ShapeDtypeStruct((feat, tgt_cells), F32),
            jax.ShapeDtypeStruct((owners, feat, feat), F32),
        ],
        in_specs=[smem] * 3 + [vmem] * 9,
        out_specs=[vmem] * 4,
        scratch_shapes=[pltpu.VMEM((src_blocks, BLK), F32), pltpu.VMEM((tgt_blocks, BLK), F32)]
        + aug
        + [pltpu.VMEM((src_blocks, feat + 8, BLK), F32), col_acc],
        compiler_params=params,
        interpret=interpret,
    )
    return sums(True), sums(False), grads


def per_device(src_emb, tgt_emb, src_hidden, growth, tgt_mass, pair_code, pair_count, block_batch):
    feat, src_cells = src_emb.shape
    tgt_cells = tgt_emb.shape[1]
    owners = ENC_DEV * lax.axis_size(("src", "tgt"))
    codes = pair_code.reshape(-1)
    count = pair_count.reshape(-1)
    first, later, grads = local_calls(codes.shape[0], feat, src_cells, tgt_cells, owners)
    growth = growth.reshape(-1, BLK)
    mass = tgt_mass.reshape(-1, BLK)
    row, col = first(codes, count, src_emb, tgt_emb)
    row, col = lax.psum(row, "tgt"), lax.psum(col, "src")
    row, col, src_log, tgt_log = later(codes, count, src_emb, tgt_emb, growth, mass, row, col)
    row, col = lax.psum(row, "tgt"), lax.psum(col, "src")
    src_pot, tgt_pot, dy, adapter = grads(
        codes, count, block_batch, src_emb, tgt_emb, src_hidden, growth, mass, row, col, src_log,
        tgt_log,
    )
    tgt_grad = lax.psum(dy, "src")
    adapter_grad = lax.psum_scatter(adapter, ("src", "tgt"), scatter_dimension=0, tiled=True)
    return src_pot.reshape(-1), tgt_pot.reshape(-1), tgt_grad, adapter_grad


def solution(mesh):
    in_specs = (
        P(None, "src"),
        P(None, "tgt"),
        P(None, "src"),
        P("src"),
        P("tgt"),
        P("src", "tgt", None),
        P("src", "tgt"),
        P("src"),
    )
    out_specs = (P("src"), P("tgt"), P(None, "tgt"), P(("src", "tgt"), None, None))
    return jax.shard_map(
        per_device, mesh=mesh, in_specs=in_specs, out_specs=out_specs, check_vma=False
    )
```

```python
import functools
import math

import jax
import jax.numpy as jnp
from jax import lax
from jax.experimental import pallas as pl
from jax.experimental.pallas import tpu as pltpu
from jax.sharding import PartitionSpec as P

BLK = 128
ENC_DEV = 1
ENTROPY = 0.5
POWER = 0.4
AUG = 16
UNROLL = 8
BF = jnp.bfloat16
F32 = jnp.float32
NT_DIMS = (((1,), (1,)), ((), ()))


def split3(value):
    high = value.astype(BF).astype(F32)
    rest = value - high
    mid = rest.astype(BF).astype(F32)
    return high, mid, rest - mid


def lanes(index):
    return pl.ds(pl.multiple_of(index * BLK, BLK), BLK)


def augment(norm_part, own_first):
    high, mid, low = split3(norm_part)
    row = lax.broadcasted_iota(jnp.int32, (AUG, BLK), 0)
    own = 0 if own_first else 3
    ones = 3 - own
    out = jnp.where((row >= ones) & (row < ones + 3), 1.0, 0.0).astype(F32)
    for place, term in enumerate((high, mid, low)):
        out = jnp.where(row == own + place, term, out)
    return out


def prepare(x_ref, y_ref, src_log, tgt_log, x_aug, y_aug, gain):
    feat = x_ref.shape[0]
    depth = x_aug.shape[1]
    src_blocks = x_ref.shape[1] // BLK
    tgt_blocks = y_ref.shape[1] // BLK

    def term(block, log_ref, index):
        norm = jnp.sum(jnp.square(block), axis=0, keepdims=True)
        value = -0.5 * norm
        if log_ref is not None:
            value = value + log_ref[pl.ds(index, 1), :] * (1.0 / gain)
        return value

    pad = jnp.zeros((depth - feat - AUG, BLK), F32)

    def src_one(index, _):
        block = x_ref[:, lanes(index)].astype(F32)
        full = jnp.concatenate([block, augment(term(block, src_log, index), True), pad], axis=0)
        x_aug[lanes(index), :] = full.T.astype(BF)
        return 0

    def tgt_one(index, _):
        bf_block = y_ref[:, lanes(index)]
        extra = augment(term(bf_block.astype(F32), tgt_log, index), False)
        y_aug[:feat, lanes(index)] = bf_block
        y_aug[feat:, lanes(index)] = jnp.concatenate([extra, pad], axis=0).astype(BF)
        return 0

    lax.fori_loop(0, src_blocks, src_one, 0, unroll=4)
    lax.fori_loop(0, tgt_blocks, tgt_one, 0, unroll=4)
    column = lax.broadcasted_iota(jnp.int32, (BLK, depth), 1)
    x_aug[pl.ds(src_blocks * BLK, BLK), :] = jnp.where(column == feat, -131072.0, 0.0).astype(BF)


def pair_of(code_ref, count, slot, src_blocks, tgt_blocks):
    code = code_ref[slot]
    shift = tgt_blocks.bit_length() - 1
    if tgt_blocks == 1 << shift:
        src_id, tgt_id = lax.shift_right_logical(code, shift), code & (tgt_blocks - 1)
    else:
        src_id, tgt_id = code // tgt_blocks, code % tgt_blocks
    return src_id, tgt_id, jnp.where(slot < count, src_id, src_blocks)


def plan_block(x_aug, y_aug, load_id, tgt_id, gain):
    acc = jnp.dot(x_aug[lanes(load_id), :], y_aug[:, lanes(tgt_id)], preferred_element_type=F32)
    return jnp.exp2(acc * (gain * math.log2(math.e)))


def split_wide(plan):
    high = plan.astype(BF)
    low = (plan - high.astype(F32)).astype(BF)
    return high, jnp.concatenate([high, low], axis=1)


def fold(plan):
    return jnp.sum(plan.reshape(BLK // 8, 8, BLK), axis=0)


def sums_kernel(first, gain, code_ref, count_ref, x_ref, y_ref, *refs):
    src_blocks = x_ref.shape[1] // BLK
    tgt_blocks = y_ref.shape[1] // BLK
    if first:
        row_out, col_out, x_aug, y_aug, row_acc, col_acc = refs
        src_log = tgt_log = None
    else:
        (growth, mass, row_in, col_in, row_out, col_out, src_log, tgt_log, x_aug, y_aug,
         row_acc, col_acc) = refs
        src_log[...] = POWER * (growth[...] - jnp.log(row_in[...]))
        tgt_log[...] = POWER * (jnp.log(mass[...]) - jnp.log(col_in[...]))
    prepare(x_ref, y_ref, src_log, tgt_log, x_aug, y_aug, gain)
    row_acc[...] = jnp.zeros_like(row_acc)
    col_acc[...] = jnp.zeros_like(col_acc)
    count = count_ref[0]
    pick = jnp.where(lax.broadcasted_iota(jnp.int32, (8, 2 * BLK), 0) == 0, 1.0, 0.0).astype(BF)

    def step(group, _):
        parts = []
        for inner in range(UNROLL):
            slot = group * UNROLL + inner
            src_id, tgt_id, load_id = pair_of(code_ref, count, slot, src_blocks, tgt_blocks)
            plan = plan_block(x_aug, y_aug, load_id, tgt_id, gain)
            _, wide = split_wide(plan)
            rows = lax.dot_general(pick, wide, NT_DIMS, preferred_element_type=F32)
            parts.append((src_id, tgt_id, rows, fold(plan)))
        for src_id, tgt_id, rows, cols in parts:
            row_acc[src_id] += rows
            col_acc[tgt_id] += cols
        return 0

    lax.fori_loop(0, (count + UNROLL - 1) // UNROLL, step, 0)
    row_out[...] = jnp.sum(row_acc[...], axis=1)
    col_out[...] = jnp.sum(col_acc[...], axis=1)


def grads_kernel(gain, code_ref, count_ref, batch_ref, x_ref, y_ref, hid_ref, growth, mass,
                 row_in, col_in, src_prev, tgt_prev, src_pot, tgt_pot, dy_ref, adp_ref,
                 src_log, tgt_log, x_aug, y_aug, dx_acc, col_acc):
    feat = x_ref.shape[0]
    src_blocks = x_ref.shape[1] // BLK
    tgt_blocks = y_ref.shape[1] // BLK
    src_new = (0.5 + POWER) * src_prev[...] + POWER * (growth[...] - jnp.log(row_in[...]))
    tgt_new = (0.5 + POWER) * tgt_prev[...] + POWER * (jnp.log(mass[...]) - jnp.log(col_in[...]))
    src_log[...] = src_new
    tgt_log[...] = tgt_new
    src_pot[...] = ENTROPY * src_new
    tgt_pot[...] = ENTROPY * tgt_new
    prepare(x_ref, y_ref, src_log, tgt_log, x_aug, y_aug, gain)
    dx_acc[...] = jnp.zeros_like(dx_acc)
    dy_ref[...] = jnp.zeros_like(dy_ref)
    col_acc[...] = jnp.zeros_like(col_acc)
    adp_ref[...] = jnp.zeros_like(adp_ref)
    count = count_ref[0]
    wide_rows = feat + AUG
    kept = feat + 8
    pick = jnp.where(
        lax.broadcasted_iota(jnp.int32, (wide_rows, BLK), 0) == feat, 1.0, 0.0
    ).astype(BF)
    group_size = UNROLL // 2

    def step(group, _):
        parts = []
        for inner in range(group_size):
            slot = group * group_size + inner
            src_id, tgt_id, load_id = pair_of(code_ref, count, slot, src_blocks, tgt_blocks)
            plan = plan_block(x_aug, y_aug, load_id, tgt_id, gain)
            high, wide = split_wide(plan)
            left = jnp.concatenate([y_aug[:wide_rows, lanes(tgt_id)], pick], axis=1)
            pulled = lax.dot_general(left, wide, NT_DIMS, preferred_element_type=F32)
            pushed = jnp.dot(x_ref[:, lanes(src_id)], high, preferred_element_type=F32)
            parts.append((src_id, tgt_id, pulled[:kept], pushed, fold(plan)))
        for src_id, tgt_id, pulled, pushed, cols in parts:
            dx_acc[src_id] += pulled
            dy_ref[:, lanes(tgt_id)] += pushed
            col_acc[tgt_id] += cols
        return 0

    lax.fori_loop(0, (count + group_size - 1) // group_size, step, 0)

    def finish_tgt(index, _):
        total = jnp.sum(col_acc[index], axis=0, keepdims=True)
        dy_ref[:, lanes(index)] = total * y_ref[:, lanes(index)].astype(F32) - dy_ref[:, lanes(index)]
        return 0

    lax.fori_loop(0, tgt_blocks, finish_tgt, 0, unroll=4)

    def finish_src(group, _):
        parts = []
        for inner in range(4):
            index = group * 4 + inner
            acc = dx_acc[index]
            grad = acc[feat:feat + 1] * x_ref[:, lanes(index)].astype(F32) - acc[:feat]
            _, wide = split_wide(grad)
            hid = hid_ref[:, lanes(index)]
            outer = lax.dot_general(
                jnp.concatenate([hid, hid], axis=1), wide, NT_DIMS, preferred_element_type=F32
            )
            parts.append((batch_ref[index], outer * (1.0 / BLK)))
        for batch, outer in parts:
            adp_ref[batch] += jnp.concatenate([outer[:feat // 2], outer[feat // 2:]], axis=1)
        return 0

    lax.fori_loop(0, src_blocks // 4, finish_src, 0)


def flip(position, bit):
    size = 1 << bit
    return position + size * (1 - 2 * ((position // size) % 2))


def greet(partners):
    barrier = pltpu.get_barrier_semaphore()
    for partner in partners:
        pl.semaphore_signal(barrier, inc=1, device_id=partner, device_id_type=pl.DeviceIdType.MESH)
    pl.semaphore_wait(barrier, len(partners))


def send(source, target, sems, slot, partner):
    copy = pltpu.make_async_remote_copy(
        src_ref=source,
        dst_ref=target,
        send_sem=sems.at[0, slot],
        recv_sem=sems.at[1, slot],
        device_id=partner,
        device_id_type=pl.DeviceIdType.MESH,
    )
    copy.start()
    return copy


def small_sums_kernel(sizes, row_in, col_in, row_out, col_out, row_got, col_got, *sems):
    axes = (
        ("tgt", row_in, row_out, row_got, sems[0], sems[1]),
        ("src", col_in, col_out, col_got, sems[2], sems[3]),
    )
    places = {axis: lax.axis_index(axis) for axis in sizes}
    greet([{axis: lax.rem(places[axis] + step, sizes[axis])} for axis in sizes
           for step in range(1, sizes[axis])])

    def share(ref, axis, owner):
        rows = ref.shape[0] // sizes[axis]
        return ref.at[pl.ds(pl.multiple_of(owner * rows, rows), rows)]

    copies = {}
    for axis, source, _, got, first, _ in axes:
        copies[axis] = []
        for step in range(1, sizes[axis]):
            peer = lax.rem(places[axis] + step, sizes[axis])
            copies[axis].append(
                send(share(source, axis, peer), got.at[step], first, step, {axis: peer})
            )
    for axis, source, out, got, _, second in axes:
        for copy in copies[axis]:
            copy.wait()
        total = share(source, axis, places[axis])[...]
        for step in range(1, sizes[axis]):
            total = total + got[step]
        share(out, axis, places[axis])[...] = total
        copies[axis] = []
        for step in range(1, sizes[axis]):
            peer = lax.rem(places[axis] + step, sizes[axis])
            mine = share(out, axis, places[axis])
            copies[axis].append(send(mine, mine, second, step, {axis: peer}))
    for axis in sizes:
        for copy in copies[axis]:
            copy.wait()


def small_sums(sizes, row, col):
    vmem = pl.BlockSpec(memory_space=pltpu.VMEM)
    scratch = []
    for axis, part in (("tgt", row), ("src", col)):
        scratch.append(pltpu.VMEM((sizes[axis], part.shape[0] // sizes[axis], BLK), F32))
    for axis in ("tgt", "src"):
        scratch += [pltpu.SemaphoreType.DMA((2, sizes[axis]))] * 2
    return pl.pallas_call(
        functools.partial(small_sums_kernel, sizes),
        out_shape=[jax.ShapeDtypeStruct(part.shape, F32) for part in (row, col)],
        in_specs=[vmem] * 2,
        out_specs=[vmem] * 2,
        scratch_shapes=scratch,
        compiler_params=pltpu.CompilerParams(collective_id=0, has_side_effects=True),
    )(row, col)


def columns(ref, start, size):
    return ref.at[:, pl.ds(pl.multiple_of(start, BLK), size)]


def add_columns(out, out_at, left, left_at, right, size):
    chunk = min(size, 8 * BLK)

    def one(index, _):
        shift = index * chunk
        columns(out, out_at + shift, chunk)[...] = (
            columns(left, left_at + shift, chunk)[...] + columns(right, shift, chunk)[...]
        )
        return 0

    lax.fori_loop(0, size // chunk, one, 0)


def last_sums_kernel(sizes, dy_in, adp_in, dy_out, adp_out, adp_sum, adp_got, *refs):
    bits = sizes["src"].bit_length() - 1
    got = (refs[:bits], refs[bits:2 * bits])
    adp_recv = refs[2 * bits:3 * bits]
    dy_sems, adp_sems, end_sems = refs[3 * bits:]
    me, mine_tgt = lax.axis_index("src"), lax.axis_index("tgt")
    tgt_peers = [lax.rem(mine_tgt + step, sizes["tgt"]) for step in range(1, sizes["tgt"])]
    greet([{"src": flip(me, bit)} for bit in range(bits)] + [{"tgt": peer} for peer in tgt_peers])
    half = dy_in.shape[1] // 2
    orders = (list(range(bits)), [0] + list(range(bits - 1, 0, -1)))
    starts = [0, half]
    sizes_now = half
    mats_start, mats = 0, adp_in.shape[0]
    history = []
    for step in range(bits):
        sizes_now //= 2
        mats //= 2
        copies, keeps, held = [], [], []
        for stream in range(2):
            bit = orders[stream][step]
            side = (me // (1 << bit)) % 2
            keep = starts[stream] + side * sizes_now
            source = dy_in if step == 0 else got[stream][step - 1]
            base = stream * half if step == 0 else 0
            copies.append(send(columns(source, base + (1 - side) * sizes_now, sizes_now),
                               got[stream][step], dy_sems, 2 * step + stream,
                               {"src": flip(me, bit)}))
            held.append((source, base + side * sizes_now))
            keeps.append(keep)
        side = (me // (1 << step)) % 2
        source = adp_in if step == 0 else adp_sum
        mats_give = mats_start + (1 - side) * mats
        mats_start = mats_start + side * mats
        copies.append(send(source.at[pl.ds(mats_give, mats)], adp_recv[step], adp_sems, step,
                           {"src": flip(me, step)}))
        for stream in range(2):
            copies[stream].wait()
            out, out_at = (got[stream][step], 0) if step < bits - 1 else (dy_out, keeps[stream])
            add_columns(out, out_at, *held[stream], got[stream][step], sizes_now)
        copies[2].wait()

        def add_mat(index, _, source=source, mats_start=mats_start, step=step):
            adp_sum[mats_start + index] = source[mats_start + index] + adp_recv[step][index]
            return 0

        lax.fori_loop(0, mats, add_mat, 0)
        history.append((keeps, sizes_now))
        starts = keeps
    ends = []
    for step, peer in enumerate(tgt_peers):
        ends.append(send(adp_sum.at[mats_start + peer], adp_got.at[step], end_sems, step,
                         {"tgt": peer}))
    for step in range(bits - 1, -1, -1):
        keeps, size = history[step]
        copies = []
        for stream in range(2):
            area = columns(dy_out, keeps[stream], size)
            copies.append(send(area, area, dy_sems, 2 * (bits + step) + stream,
                               {"src": flip(me, orders[stream][step])}))
        for copy in copies:
            copy.wait()
    total = adp_sum[mats_start + mine_tgt]
    for step, copy in enumerate(ends):
        copy.wait()
        total = total + adp_got[step]
    adp_out[...] = total


def last_sums(sizes, dy, adapter):
    bits = sizes["src"].bit_length() - 1
    vmem = pl.BlockSpec(memory_space=pltpu.VMEM)
    feat, cells = dy.shape
    owners, mat_rows, mat_cols = adapter.shape
    parts = [pltpu.VMEM((feat, cells >> (step + 2)), F32) for step in range(bits)]
    mats = [pltpu.VMEM((owners >> (step + 1), mat_rows, mat_cols), F32) for step in range(bits)]
    return pl.pallas_call(
        functools.partial(last_sums_kernel, sizes),
        out_shape=[
            jax.ShapeDtypeStruct(dy.shape, F32),
            jax.ShapeDtypeStruct((mat_rows, mat_cols), F32),
        ],
        in_specs=[vmem] * 2,
        out_specs=[vmem] * 2,
        scratch_shapes=[
            pltpu.VMEM(adapter.shape, F32),
            pltpu.VMEM((max(sizes["tgt"] - 1, 1), mat_rows, mat_cols), F32),
        ]
        + parts * 2
        + mats
        + [
            pltpu.SemaphoreType.DMA((2, 4 * bits)),
            pltpu.SemaphoreType.DMA((2, bits)),
            pltpu.SemaphoreType.DMA((2, max(sizes["tgt"] - 1, 1))),
        ],
        compiler_params=pltpu.CompilerParams(
            collective_id=1, has_side_effects=True, vmem_limit_bytes=40 * 1024 * 1024
        ),
    )(dy, adapter)


def local_calls(slots, feat, src_cells, tgt_cells, owners, interpret=False):
    src_blocks, tgt_blocks = src_cells // BLK, tgt_cells // BLK
    gain = 2.0 / (feat * ENTROPY)
    depth = -(-(feat + AUG) // BLK) * BLK
    smem = pl.BlockSpec(memory_space=pltpu.SMEM)
    vmem = pl.BlockSpec(memory_space=pltpu.VMEM)
    row_shape = jax.ShapeDtypeStruct((src_blocks, BLK), F32)
    col_shape = jax.ShapeDtypeStruct((tgt_blocks, BLK), F32)
    aug = [pltpu.VMEM((src_cells + BLK, depth), BF), pltpu.VMEM((depth, tgt_cells), BF)]
    col_acc = pltpu.VMEM((tgt_blocks, 8, BLK), F32)
    params = pltpu.CompilerParams(vmem_limit_bytes=56 * 1024 * 1024)

    def sums(first):
        scratch = aug + [pltpu.VMEM((src_blocks, 8, BLK), F32), col_acc]
        outs = [row_shape, col_shape] + ([] if first else [row_shape, col_shape])
        return pl.pallas_call(
            functools.partial(sums_kernel, first, gain),
            out_shape=outs,
            in_specs=[smem] * 2 + [vmem] * (2 if first else 6),
            out_specs=[vmem] * len(outs),
            scratch_shapes=scratch,
            compiler_params=params,
            interpret=interpret,
        )

    grads = pl.pallas_call(
        functools.partial(grads_kernel, gain),
        out_shape=[
            row_shape,
            col_shape,
            jax.ShapeDtypeStruct((feat, tgt_cells), F32),
            jax.ShapeDtypeStruct((owners, feat // 2, 2 * feat), F32),
        ],
        in_specs=[smem] * 3 + [vmem] * 9,
        out_specs=[vmem] * 4,
        scratch_shapes=[pltpu.VMEM((src_blocks, BLK), F32), pltpu.VMEM((tgt_blocks, BLK), F32)]
        + aug
        + [pltpu.VMEM((src_blocks, feat + 8, BLK), F32), col_acc],
        compiler_params=params,
        interpret=interpret,
    )
    return sums(True), sums(False), grads


def per_device(src_emb, tgt_emb, src_hidden, growth, tgt_mass, pair_code, pair_count, block_batch):
    feat, src_cells = src_emb.shape
    tgt_cells = tgt_emb.shape[1]
    owners = ENC_DEV * lax.axis_size(("src", "tgt"))
    codes = pair_code.reshape(-1)
    count = pair_count.reshape(-1)
    first, later, grads = local_calls(codes.shape[0], feat, src_cells, tgt_cells, owners)
    growth = growth.reshape(-1, BLK)
    mass = tgt_mass.reshape(-1, BLK)
    sizes = {axis: lax.axis_size(axis) for axis in ("src", "tgt")}
    bits = sizes["src"].bit_length() - 1
    owner_src = block_batch // sizes["tgt"]
    spot = sum((owner_src // (1 << bit)) % 2 * (1 << (bits - 1 - bit)) for bit in range(bits))
    spots = spot * sizes["tgt"] + block_batch % sizes["tgt"]
    row, col = small_sums(sizes, *first(codes, count, src_emb, tgt_emb))
    row, col, src_log, tgt_log = later(codes, count, src_emb, tgt_emb, growth, mass, row, col)
    row, col = small_sums(sizes, row, col)
    src_pot, tgt_pot, dy, adapter = grads(
        codes, count, spots, src_emb, tgt_emb, src_hidden, growth, mass, row, col, src_log,
        tgt_log,
    )
    tgt_grad, packed = last_sums(sizes, dy, adapter)
    adapter_grad = jnp.concatenate([packed[:, :feat], packed[:, feat:]], axis=0)[None]
    return src_pot.reshape(-1), tgt_pot.reshape(-1), tgt_grad, adapter_grad


def solution(mesh):
    in_specs = (
        P(None, "src"),
        P(None, "tgt"),
        P(None, "src"),
        P("src"),
        P("tgt"),
        P("src", "tgt", None),
        P("src", "tgt"),
        P("src"),
    )
    out_specs = (P("src"), P("tgt"), P(None, "tgt"), P(("src", "tgt"), None, None))
    return jax.shard_map(
        per_device, mesh=mesh, in_specs=in_specs, out_specs=out_specs, check_vma=False
    )
```

```python
import functools
import math

import jax
import jax.numpy as jnp
from jax import lax
from jax.experimental import pallas as pl
from jax.experimental.pallas import tpu as pltpu
from jax.sharding import PartitionSpec as P

BLK = 128
ENC_DEV = 1
ENTROPY = 0.5
POWER = 0.4
AUG = 16
UNROLL = 16
BF = jnp.bfloat16
F32 = jnp.float32


def split3(value):
    high = value.astype(BF).astype(F32)
    rest = value - high
    mid = rest.astype(BF).astype(F32)
    return high, mid, rest - mid


def lanes(index):
    return pl.ds(pl.multiple_of(index * BLK, BLK), BLK)


def augment(norm_part, own_first):
    high, mid, low = split3(norm_part)
    row = lax.broadcasted_iota(jnp.int32, (AUG, BLK), 0)
    own = 0 if own_first else 3
    ones = 3 - own
    out = jnp.where((row >= ones) & (row < ones + 3), 1.0, 0.0).astype(F32)
    for place, term in enumerate((high, mid, low)):
        out = jnp.where(row == own + place, term, out)
    return out


def prepare(x_ref, y_ref, src_log, tgt_log, x_aug, y_aug, gain, y_turned=None):
    feat = x_ref.shape[0]
    depth = x_aug.shape[1]
    src_blocks = x_ref.shape[1] // BLK
    tgt_blocks = y_ref.shape[1] // BLK

    def term(block, log_ref, index):
        norm = jnp.sum(jnp.square(block), axis=0, keepdims=True)
        value = -0.5 * norm
        if log_ref is not None:
            value = value + log_ref[pl.ds(index, 1), :] * (1.0 / gain)
        return value

    pad = jnp.zeros((depth - feat - AUG, BLK), F32)

    def src_one(index, _):
        block = x_ref[:, lanes(index)].astype(F32)
        full = jnp.concatenate([block, augment(term(block, src_log, index), True), pad], axis=0)
        x_aug[lanes(index), :] = full.T.astype(BF)
        return 0

    def tgt_one(index, _):
        bf_block = y_ref[:, lanes(index)]
        extra = augment(term(bf_block.astype(F32), tgt_log, index), False)
        y_aug[:feat, lanes(index)] = bf_block
        y_aug[feat:, lanes(index)] = jnp.concatenate([extra, pad], axis=0).astype(BF)
        if y_turned is not None:
            full = jnp.concatenate([bf_block.astype(F32), extra, pad], axis=0)
            y_turned[lanes(index), :] = full.T.astype(BF)
        return 0

    lax.fori_loop(0, src_blocks, src_one, 0, unroll=8)
    lax.fori_loop(0, tgt_blocks, tgt_one, 0, unroll=8)
    column = lax.broadcasted_iota(jnp.int32, (BLK, depth), 1)
    x_aug[pl.ds(src_blocks * BLK, BLK), :] = jnp.where(column == feat, -131072.0, 0.0).astype(BF)


def pair_of(code_ref, count, slot, src_blocks, tgt_blocks):
    code = code_ref[slot]
    shift = tgt_blocks.bit_length() - 1
    if tgt_blocks == 1 << shift:
        src_id, tgt_id = lax.shift_right_logical(code, shift), code & (tgt_blocks - 1)
    else:
        src_id, tgt_id = code // tgt_blocks, code % tgt_blocks
    return src_id, tgt_id, jnp.where(slot < count, src_id, src_blocks)


def plan_block(x_aug, y_aug, load_id, tgt_id, gain):
    acc = jnp.dot(x_aug[lanes(load_id), :], y_aug[:, lanes(tgt_id)], preferred_element_type=F32)
    return jnp.exp2(acc * (gain * math.log2(math.e)))


def fold(plan):
    return jnp.sum(plan.reshape(BLK // 8, 8, BLK), axis=0)


def sums_kernel(first, gain, code_ref, count_ref, x_ref, y_ref, *refs):
    src_blocks = x_ref.shape[1] // BLK
    tgt_blocks = y_ref.shape[1] // BLK
    if first:
        row_out, col_out, x_aug, y_aug, row_acc, col_acc = refs
        src_log = tgt_log = None
    else:
        (growth, mass, row_in, col_in, row_out, col_out, src_log, tgt_log, x_aug, y_aug,
         row_acc, col_acc) = refs
        src_log[...] = POWER * (growth[...] - jnp.log(row_in[...]))
        tgt_log[...] = POWER * (jnp.log(mass[...]) - jnp.log(col_in[...]))
    prepare(x_ref, y_ref, src_log, tgt_log, x_aug, y_aug, gain)
    row_acc[...] = jnp.zeros_like(row_acc)
    col_acc[...] = jnp.zeros_like(col_acc)
    count = count_ref[0]
    def step(group, _):
        parts = []
        for inner in range(UNROLL):
            slot = group * UNROLL + inner
            src_id, tgt_id, load_id = pair_of(code_ref, count, slot, src_blocks, tgt_blocks)
            plan = plan_block(x_aug, y_aug, load_id, tgt_id, gain)
            parts.append((src_id, tgt_id, jnp.sum(plan, axis=1, keepdims=True), fold(plan)))
        for src_id, tgt_id, rows, cols in parts:
            row_acc[src_id] = row_acc[src_id] + rows
            col_acc[tgt_id] += cols
        return 0

    lax.fori_loop(0, (count + UNROLL - 1) // UNROLL, step, 0)
    diagonal = lax.broadcasted_iota(jnp.int32, (BLK, BLK), 0) == lax.broadcasted_iota(
        jnp.int32, (BLK, BLK), 1
    )

    def lay_flat(index, _):
        row_out[pl.ds(index, 1), :] = jnp.sum(
            jnp.where(diagonal, row_acc[index], 0.0), axis=0, keepdims=True
        )
        return 0

    lax.fori_loop(0, src_blocks, lay_flat, 0, unroll=8)
    col_out[...] = jnp.sum(col_acc[...], axis=1)


def grads_kernel(gain, code_ref, count_ref, batch_ref, x_ref, y_ref, hid_ref, growth, mass,
                 row_in, col_in, src_prev, tgt_prev, src_pot, tgt_pot, dy_ref, adp_ref,
                 src_log, tgt_log, x_aug, y_aug, y_turned, dx_acc, col_acc):
    feat = x_ref.shape[0]
    src_blocks = x_ref.shape[1] // BLK
    tgt_blocks = y_ref.shape[1] // BLK
    src_new = (0.5 + POWER) * src_prev[...] + POWER * (growth[...] - jnp.log(row_in[...]))
    tgt_new = (0.5 + POWER) * tgt_prev[...] + POWER * (jnp.log(mass[...]) - jnp.log(col_in[...]))
    src_log[...] = src_new
    tgt_log[...] = tgt_new
    src_pot[...] = ENTROPY * src_new
    tgt_pot[...] = ENTROPY * tgt_new
    prepare(x_ref, y_ref, src_log, tgt_log, x_aug, y_aug, gain, y_turned)
    dx_acc[...] = jnp.zeros_like(dx_acc)
    dy_ref[...] = jnp.zeros_like(dy_ref)
    col_acc[...] = jnp.zeros_like(col_acc)
    adp_ref[...] = jnp.zeros_like(adp_ref)
    count = count_ref[0]
    is_sum = lax.broadcasted_iota(jnp.int32, (BLK, x_aug.shape[1]), 1) == feat
    group_size = UNROLL // 2

    def step(group, _):
        parts = []
        for inner in range(group_size):
            slot = group * group_size + inner
            src_id, tgt_id, load_id = pair_of(code_ref, count, slot, src_blocks, tgt_blocks)
            plan = plan_block(x_aug, y_aug, load_id, tgt_id, gain)
            parts.append((src_id, tgt_id, plan.astype(BF), jnp.sum(plan, axis=1, keepdims=True)))
            col_acc[tgt_id] += fold(plan)
        for src_id, tgt_id, high, rows in parts:
            pulled = jnp.dot(high, y_turned[lanes(tgt_id), :], preferred_element_type=F32)
            dx_acc[src_id] += jnp.where(is_sum, rows, pulled)
        for src_id, tgt_id, high, rows in parts:
            dy_ref[:, lanes(tgt_id)] += jnp.dot(
                x_ref[:, lanes(src_id)], high, preferred_element_type=F32
            )
        return 0

    lax.fori_loop(0, (count + group_size - 1) // group_size, step, 0)

    def finish_tgt(index, _):
        total = jnp.sum(col_acc[index], axis=0, keepdims=True)
        dy_ref[:, lanes(index)] = total * y_ref[:, lanes(index)].astype(F32) - dy_ref[:, lanes(index)]
        return 0

    lax.fori_loop(0, tgt_blocks, finish_tgt, 0, unroll=8)

    def finish_src(group, _):
        parts = []
        for inner in range(4):
            index = group * 4 + inner
            acc = dx_acc[index]
            turned = x_aug[lanes(index), :].astype(F32)
            grad = (acc[:, feat:feat + 1] * turned - acc)[:, :feat]
            high = grad.astype(BF)
            both = jnp.concatenate([high, (grad - high.astype(F32)).astype(BF)], axis=0)
            hid = hid_ref[:, lanes(index)]
            outer = jnp.dot(
                jnp.concatenate([hid, hid], axis=1), both, preferred_element_type=F32
            )
            parts.append((batch_ref[index], outer * (1.0 / BLK)))
        for batch, outer in parts:
            adp_ref[batch] += jnp.concatenate([outer[:feat // 2], outer[feat // 2:]], axis=1)
        return 0

    lax.fori_loop(0, src_blocks // 4, finish_src, 0)


def flip(position, bit):
    size = 1 << bit
    return position + size * (1 - 2 * ((position // size) % 2))


def greet(partners):
    barrier = pltpu.get_barrier_semaphore()
    for partner in partners:
        pl.semaphore_signal(barrier, inc=1, device_id=partner, device_id_type=pl.DeviceIdType.MESH)
    pl.semaphore_wait(barrier, len(partners))


def send(source, target, sems, slot, partner):
    copy = pltpu.make_async_remote_copy(
        src_ref=source,
        dst_ref=target,
        send_sem=sems.at[0, slot],
        recv_sem=sems.at[1, slot],
        device_id=partner,
        device_id_type=pl.DeviceIdType.MESH,
    )
    copy.start()
    return copy


def small_sums_kernel(sizes, row_in, col_in, row_out, col_out, row_got, col_got, *sems):
    axes = (
        ("tgt", row_in, row_out, row_got, sems[0], sems[1]),
        ("src", col_in, col_out, col_got, sems[2], sems[3]),
    )
    places = {axis: lax.axis_index(axis) for axis in sizes}
    greet([{axis: lax.rem(places[axis] + step, sizes[axis])} for axis in sizes
           for step in range(1, sizes[axis])])

    def share(ref, axis, owner):
        rows = ref.shape[0] // sizes[axis]
        return ref.at[pl.ds(pl.multiple_of(owner * rows, rows), rows)]

    copies = {}
    for axis, source, _, got, first, _ in axes:
        copies[axis] = []
        for step in range(1, sizes[axis]):
            peer = lax.rem(places[axis] + step, sizes[axis])
            copies[axis].append(
                send(share(source, axis, peer), got.at[step], first, step, {axis: peer})
            )
    for axis, source, out, got, _, second in axes:
        for copy in copies[axis]:
            copy.wait()
        total = share(source, axis, places[axis])[...]
        for step in range(1, sizes[axis]):
            total = total + got[step]
        share(out, axis, places[axis])[...] = total
        copies[axis] = []
        for step in range(1, sizes[axis]):
            peer = lax.rem(places[axis] + step, sizes[axis])
            mine = share(out, axis, places[axis])
            copies[axis].append(send(mine, mine, second, step, {axis: peer}))
    for axis in sizes:
        for copy in copies[axis]:
            copy.wait()


def small_sums(sizes, row, col):
    vmem = pl.BlockSpec(memory_space=pltpu.VMEM)
    scratch = []
    for axis, part in (("tgt", row), ("src", col)):
        scratch.append(pltpu.VMEM((sizes[axis], part.shape[0] // sizes[axis], BLK), F32))
    for axis in ("tgt", "src"):
        scratch += [pltpu.SemaphoreType.DMA((2, sizes[axis]))] * 2
    return pl.pallas_call(
        functools.partial(small_sums_kernel, sizes),
        out_shape=[jax.ShapeDtypeStruct(part.shape, F32) for part in (row, col)],
        in_specs=[vmem] * 2,
        out_specs=[vmem] * 2,
        scratch_shapes=scratch,
        compiler_params=pltpu.CompilerParams(collective_id=0, has_side_effects=True),
    )(row, col)


def columns(ref, start, size):
    return ref.at[:, pl.ds(pl.multiple_of(start, BLK), size)]


def add_columns(out, out_at, left, left_at, right, size):
    chunk = min(size, 8 * BLK)

    def one(index, _):
        shift = index * chunk
        columns(out, out_at + shift, chunk)[...] = (
            columns(left, left_at + shift, chunk)[...] + columns(right, shift, chunk)[...]
        )
        return 0

    lax.fori_loop(0, size // chunk, one, 0)


def last_sums_kernel(sizes, dy_in, adp_in, dy_out, adp_out, adp_sum, adp_got, *refs):
    bits = sizes["src"].bit_length() - 1
    got = (refs[:bits], refs[bits:2 * bits])
    adp_recv = refs[2 * bits:3 * bits]
    dy_sems, adp_sems, end_sems = refs[3 * bits:]
    me, mine_tgt = lax.axis_index("src"), lax.axis_index("tgt")
    tgt_peers = [lax.rem(mine_tgt + step, sizes["tgt"]) for step in range(1, sizes["tgt"])]
    greet([{"src": flip(me, bit)} for bit in range(bits)] + [{"tgt": peer} for peer in tgt_peers])
    half = dy_in.shape[1] // 2
    orders = (list(range(bits)), [0] + list(range(bits - 1, 0, -1)))
    starts = [0, half]
    sizes_now = half
    mats_start, mats = 0, adp_in.shape[0]
    history = []
    for step in range(bits):
        sizes_now //= 2
        mats //= 2
        copies, keeps, held = [], [], []
        for stream in range(2):
            bit = orders[stream][step]
            side = (me // (1 << bit)) % 2
            keep = starts[stream] + side * sizes_now
            source = dy_in if step == 0 else got[stream][step - 1]
            base = stream * half if step == 0 else 0
            copies.append(send(columns(source, base + (1 - side) * sizes_now, sizes_now),
                               got[stream][step], dy_sems, 2 * step + stream,
                               {"src": flip(me, bit)}))
            held.append((source, base + side * sizes_now))
            keeps.append(keep)
        side = (me // (1 << step)) % 2
        source = adp_in if step == 0 else adp_sum
        mats_give = mats_start + (1 - side) * mats
        mats_start = mats_start + side * mats
        copies.append(send(source.at[pl.ds(mats_give, mats)], adp_recv[step], adp_sems, step,
                           {"src": flip(me, step)}))
        for stream in range(2):
            copies[stream].wait()
            out, out_at = (got[stream][step], 0) if step < bits - 1 else (dy_out, keeps[stream])
            add_columns(out, out_at, *held[stream], got[stream][step], sizes_now)
        copies[2].wait()

        def add_mat(index, _, source=source, mats_start=mats_start, step=step):
            adp_sum[mats_start + index] = source[mats_start + index] + adp_recv[step][index]
            return 0

        lax.fori_loop(0, mats, add_mat, 0)
        history.append((keeps, sizes_now))
        starts = keeps
    ends = []
    for step, peer in enumerate(tgt_peers):
        ends.append(send(adp_sum.at[mats_start + peer], adp_got.at[step], end_sems, step,
                         {"tgt": peer}))
    for step in range(bits - 1, -1, -1):
        keeps, size = history[step]
        copies = []
        for stream in range(2):
            area = columns(dy_out, keeps[stream], size)
            copies.append(send(area, area, dy_sems, 2 * (bits + step) + stream,
                               {"src": flip(me, orders[stream][step])}))
        for copy in copies:
            copy.wait()
    total = adp_sum[mats_start + mine_tgt]
    for step, copy in enumerate(ends):
        copy.wait()
        total = total + adp_got[step]
    adp_out[...] = total


def last_sums(sizes, dy, adapter):
    bits = sizes["src"].bit_length() - 1
    vmem = pl.BlockSpec(memory_space=pltpu.VMEM)
    feat, cells = dy.shape
    owners, mat_rows, mat_cols = adapter.shape
    parts = [pltpu.VMEM((feat, cells >> (step + 2)), F32) for step in range(bits)]
    mats = [pltpu.VMEM((owners >> (step + 1), mat_rows, mat_cols), F32) for step in range(bits)]
    return pl.pallas_call(
        functools.partial(last_sums_kernel, sizes),
        out_shape=[
            jax.ShapeDtypeStruct(dy.shape, F32),
            jax.ShapeDtypeStruct((mat_rows, mat_cols), F32),
        ],
        in_specs=[vmem] * 2,
        out_specs=[vmem] * 2,
        scratch_shapes=[
            pltpu.VMEM(adapter.shape, F32),
            pltpu.VMEM((max(sizes["tgt"] - 1, 1), mat_rows, mat_cols), F32),
        ]
        + parts * 2
        + mats
        + [
            pltpu.SemaphoreType.DMA((2, 4 * bits)),
            pltpu.SemaphoreType.DMA((2, bits)),
            pltpu.SemaphoreType.DMA((2, max(sizes["tgt"] - 1, 1))),
        ],
        compiler_params=pltpu.CompilerParams(
            collective_id=1, has_side_effects=True, vmem_limit_bytes=40 * 1024 * 1024
        ),
    )(dy, adapter)


def local_calls(slots, feat, src_cells, tgt_cells, owners, interpret=False):
    src_blocks, tgt_blocks = src_cells // BLK, tgt_cells // BLK
    gain = 2.0 / (feat * ENTROPY)
    depth = -(-(feat + AUG) // BLK) * BLK
    smem = pl.BlockSpec(memory_space=pltpu.SMEM)
    vmem = pl.BlockSpec(memory_space=pltpu.VMEM)
    row_shape = jax.ShapeDtypeStruct((src_blocks, BLK), F32)
    col_shape = jax.ShapeDtypeStruct((tgt_blocks, BLK), F32)
    aug = [pltpu.VMEM((src_cells + BLK, depth), BF), pltpu.VMEM((depth, tgt_cells), BF)]
    col_acc = pltpu.VMEM((tgt_blocks, 8, BLK), F32)
    params = pltpu.CompilerParams(vmem_limit_bytes=56 * 1024 * 1024)

    def sums(first):
        scratch = aug + [pltpu.VMEM((src_blocks, BLK, BLK), F32), col_acc]
        outs = [row_shape, col_shape] + ([] if first else [row_shape, col_shape])
        return pl.pallas_call(
            functools.partial(sums_kernel, first, gain),
            out_shape=outs,
            in_specs=[smem] * 2 + [vmem] * (2 if first else 6),
            out_specs=[vmem] * len(outs),
            scratch_shapes=scratch,
            compiler_params=params,
            interpret=interpret,
        )

    grads = pl.pallas_call(
        functools.partial(grads_kernel, gain),
        out_shape=[
            row_shape,
            col_shape,
            jax.ShapeDtypeStruct((feat, tgt_cells), F32),
            jax.ShapeDtypeStruct((owners, feat // 2, 2 * feat), F32),
        ],
        in_specs=[smem] * 3 + [vmem] * 9,
        out_specs=[vmem] * 4,
        scratch_shapes=[pltpu.VMEM((src_blocks, BLK), F32), pltpu.VMEM((tgt_blocks, BLK), F32)]
        + aug
        + [
            pltpu.VMEM((tgt_cells, depth), BF),
            pltpu.VMEM((src_blocks, BLK, depth), F32),
            col_acc,
        ],
        compiler_params=params,
        interpret=interpret,
    )
    return sums(True), sums(False), grads


def per_device(src_emb, tgt_emb, src_hidden, growth, tgt_mass, pair_code, pair_count, block_batch):
    feat, src_cells = src_emb.shape
    tgt_cells = tgt_emb.shape[1]
    owners = ENC_DEV * lax.axis_size(("src", "tgt"))
    codes = pair_code.reshape(-1)
    count = pair_count.reshape(-1)
    first, later, grads = local_calls(codes.shape[0], feat, src_cells, tgt_cells, owners)
    growth = growth.reshape(-1, BLK)
    mass = tgt_mass.reshape(-1, BLK)
    sizes = {axis: lax.axis_size(axis) for axis in ("src", "tgt")}
    bits = sizes["src"].bit_length() - 1
    owner_src = block_batch // sizes["tgt"]
    spot = sum((owner_src // (1 << bit)) % 2 * (1 << (bits - 1 - bit)) for bit in range(bits))
    spots = spot * sizes["tgt"] + block_batch % sizes["tgt"]
    row, col = small_sums(sizes, *first(codes, count, src_emb, tgt_emb))
    row, col, src_log, tgt_log = later(codes, count, src_emb, tgt_emb, growth, mass, row, col)
    row, col = small_sums(sizes, row, col)
    src_pot, tgt_pot, dy, adapter = grads(
        codes, count, spots, src_emb, tgt_emb, src_hidden, growth, mass, row, col, src_log,
        tgt_log,
    )
    tgt_grad, packed = last_sums(sizes, dy, adapter)
    adapter_grad = jnp.concatenate([packed[:, :feat], packed[:, feat:]], axis=0)[None]
    return src_pot.reshape(-1), tgt_pot.reshape(-1), tgt_grad, adapter_grad


def solution(mesh):
    in_specs = (
        P(None, "src"),
        P(None, "tgt"),
        P(None, "src"),
        P("src"),
        P("tgt"),
        P("src", "tgt", None),
        P("src", "tgt"),
        P("src"),
    )
    out_specs = (P("src"), P("tgt"), P(None, "tgt"), P(("src", "tgt"), None, None))
    return jax.shard_map(
        per_device, mesh=mesh, in_specs=in_specs, out_specs=out_specs, check_vma=False
    )
```
